256 devices in a mesh: term: 32 (over z_hi, x, core), sector: 8 (over y, z_lo).
Axes of the slice: x: 4, y: 4, z: 8 (z_hi: 4, z_lo: 2; z = z_hi * 2 + z_lo), core: 2. Of those that a mesh axis runs over, the one named last changes fastest.
Arguments:
- wave: float32 [8, 512, 512], P('sector', 'term'), may hold values from -6 to 6
- left_ops: bfloat16 [256, 8, 512, 512], P('term', 'sector'), may hold values from -1 to 1
- right_ops: bfloat16 [256, 8, 512, 512], P('term', 'sector'), may hold values from -4 to 1
- diagonal: float32 [8, 512, 512], P('sector', 'term'), may hold values from -21 to 0
- block_size: int32 [8], replicated, may hold values from 128 to 512, as said below
- source: int32 [256, 8], P('term'), may hold values from 0 to 7, as said below
Outputs:
- new_vector: float32 [8, 512, 512], P('sector', 'term')
- new_sigma: float32 [8, 512, 512], P('sector', 'term')
- subspace: float32 [2, 2], replicated
The draws below stay inside these ranges and needn't reach their ends.
Inputs may be any that keep to these rules, and one draw needn't show every extreme that they name: `block_size`: every block size lies between 128 and 512; some sector has exactly 512. `source`: entries name sectors.
All inputs are finite; a program needn't handle non-finite values.
Results may differ from the reference program's by a relative error of at most 0.005.
Values may be sent and summed in bfloat16 or wider, within the bound.
A program may use at most 64 MiB of HBM per device.

```python
import math
import jax
import jax.numpy as jnp
from jax import lax

B = 512
TERMS = 256
NSEC = 8


def draw_block_size(key, part):
    key_sizes = jax.random.fold_in(key, 11)
    key_place = jax.random.fold_in(key, 23)
    sizes = jax.random.randint(key_sizes, (NSEC,), B // 4, B + 1).astype(jnp.int32)
    place = jax.random.randint(key_place, (), 0, NSEC).astype(jnp.int32)
    return jnp.where(jnp.arange(NSEC).astype(jnp.int32) == place, B, sizes).astype(jnp.int32)


def sector_sources(key):
    key_keep = jax.random.fold_in(key, 101)
    key_offset = jax.random.fold_in(key, 103)
    keep_sector = jax.random.randint(key_keep, (TERMS, NSEC), 0, 2).astype(jnp.int32)
    offset_step = jax.random.randint(key_offset, (TERMS, NSEC), 1, NSEC).astype(jnp.int32)
    targets = jnp.arange(NSEC).astype(jnp.int32)[None, :]
    return jnp.where(keep_sector == 1, targets, (targets + offset_step) % NSEC).astype(jnp.int32)


def right_scale(key):
    key_scale = jax.random.fold_in(key, 107)
    return jnp.exp(jax.random.uniform(key_scale, (NSEC, B), jnp.float32, math.log(0.25), math.log(2.5)))


def unit_noise(key_noise, shape):
    return jnp.clip(jax.random.normal(key_noise, shape, jnp.float32), -6.0, 6.0)


def draw_source(key, part):
    return sector_sources(key)


def draw_left_ops(key, part):
    sources = sector_sources(key)
    noise = unit_noise(jax.random.fold_in(key, 109), (TERMS, NSEC, B, B)) * (1.0 / math.sqrt(B * TERMS))
    targets = jnp.arange(NSEC).astype(jnp.int32)[None, :]
    shift = jnp.where(sources == targets, 6.0 / TERMS, 0.0).astype(jnp.float32)
    rows = jnp.arange(B).astype(jnp.int32)
    on_diagonal = rows[:, None] == rows[None, :]
    return jnp.where(on_diagonal[None, None], noise + shift[:, :, None, None], noise).astype(jnp.bfloat16)


def draw_right_ops(key, part):
    scale = right_scale(key)
    noise = unit_noise(jax.random.fold_in(key, 111), (TERMS, NSEC, B, B)) * (1.0 / math.sqrt(B))
    rows = jnp.arange(B).astype(jnp.int32)
    on_diagonal = rows[:, None] == rows[None, :]
    return jnp.where(on_diagonal[None, None], noise - scale[None, :, None, :], noise).astype(jnp.bfloat16)


def draw_diagonal(key, part):
    sources = sector_sources(key)
    targets = jnp.arange(NSEC).astype(jnp.int32)[None, :]
    counts = jnp.sum((sources == targets).astype(jnp.int32), axis=0)
    coeff = 6.0 / TERMS * counts.astype(jnp.float32)
    scale = right_scale(key)
    key_noise = jax.random.fold_in(key, 113)
    sector_offset = jax.random.uniform(jax.random.fold_in(key, 117), (NSEC,), jnp.float32, -4.0, -2.0)
    noise = jax.random.uniform(key_noise, (NSEC, B, B), jnp.float32, -1.5, 1.5)
    return (noise - coeff[:, None, None] * scale[:, None, :] + sector_offset[:, None, None]).astype(jnp.float32)


def block_levels(rng, dims, cuts, least, high):
    level = 1.0
    for axis_at, shards_of in cuts:
        draws = jax.random.uniform(jax.random.fold_in(jax.random.fold_in(rng, 6), axis_at), (shards_of,), jnp.float32, least / len(cuts), high / len(cuts))
        level = level * jnp.repeat(jnp.exp(draws), dims[axis_at] // shards_of).reshape((-1,) + (1,) * (len(dims) - 1 - axis_at))
    return level


def gaussian(stream_key, dims, spread, reach, cuts=(), held_as=jnp.bfloat16):
    gain = block_levels(stream_key, dims, cuts, -0.22, 0.18) if cuts else 1.0
    array = jax.random.normal(stream_key, dims, jnp.float32) * spread * gain
    return jnp.minimum(jnp.maximum(array, -reach), reach).astype(held_as)


def setup_inputs(seed: int = 0) -> dict:
    splits = jax.random.split(jax.random.key(seed), 7)
    wave = gaussian(splits[0], (NSEC, B, B), 1.0, 6.0, ((0, 8), (1, 32)), jnp.float32)
    left_ops = draw_left_ops(jax.random.fold_in(splits[6], 71), 0)
    right_ops = draw_right_ops(jax.random.fold_in(splits[6], 71), 0)
    diagonal = draw_diagonal(jax.random.fold_in(splits[6], 71), 0)
    block_size = draw_block_size(jax.random.fold_in(splits[6], 71), 0)
    source = draw_source(jax.random.fold_in(splits[6], 71), 0)
    return {"wave": wave, "left_ops": left_ops, "right_ops": right_ops, "diagonal": diagonal, "block_size": block_size, "source": source}


def reference(wave, left_ops, right_ops, diagonal, block_size, source):
    total = float(NSEC * B * B)
    index = jnp.arange(B).astype(jnp.int32)
    valid = ((index[None, :, None] < block_size[:, None, None]) & (index[None, None, :] < block_size[:, None, None])).astype(jnp.float32)
    masked = wave * valid
    first_vec = masked / jnp.sqrt(jnp.sum(masked * masked) / total + 1e-06)

    def apply_ham(vector):
        vector_b = vector.astype(jnp.bfloat16)

        def step(accum, item):
            left, right, src_row = item
            blocks = jnp.take(vector_b, src_row, axis=0)
            halfway = jnp.einsum('pij,pjk->pik', left.astype(jnp.float32), blocks.astype(jnp.float32)).astype(jnp.bfloat16)
            return (accum + jnp.einsum('pij,pkj->pik', halfway.astype(jnp.float32), right.astype(jnp.float32)), None)
        start_acc = jnp.zeros((NSEC, B, B), jnp.float32)
        summed, unused = lax.scan(step, start_acc, (left_ops, right_ops, source))
        return summed * valid
    first_sigma = apply_ham(first_vec)
    theta = jnp.sum(first_vec * first_sigma) / total
    correction = (first_sigma - theta * first_vec) / jnp.maximum(jnp.abs(diagonal - theta), 1.0)
    correlation = jnp.sum(first_vec * correction) / total
    orth = correction - correlation * first_vec
    new_vector = orth / jnp.sqrt(jnp.sum(orth * orth) / total + 1e-06)
    new_sigma = apply_ham(new_vector)
    upper = jnp.sum(first_vec * new_sigma) / total
    lower = jnp.sum(new_vector * first_sigma) / total
    corner = jnp.sum(new_vector * new_sigma) / total
    subspace = jnp.stack([jnp.stack([theta, upper]), jnp.stack([lower, corner])]).astype(jnp.float32)
    return (new_vector, new_sigma, subspace)
```

```python
import jax
import jax.numpy as jnp
from jax import lax
from jax.experimental import pallas as pl
from jax.experimental.pallas import tpu as pltpu
from jax.sharding import PartitionSpec as P

MESH = pl.DeviceIdType.MESH
F32 = jnp.float32
BF16 = jnp.bfloat16

NX, NY, NZH, NZL, NC = 4, 4, 4, 2, 2
NZ = NZH * NZL

AG_FIRST = 0
AG_ZR = 3
AG_ZL = 7
AG_GR = 11
AG_GL = 19
AG_HR = 27
AG_HL = 35
AG_M = 43
RS_C = 75
RS = 76
AR1 = 92
AR2 = 100
AR3 = 104
NSEM = 112


def device(x, y, z, c):
    return {"term": (z // NZL) * (NX * NC) + x * NC + c, "sector": y * NZL + z % NZL}


def kernel(
    total,
    bs_ref,
    source_ref,
    wave_ref,
    diag_ref,
    left_hbm,
    right_hbm,
    vec_ref,
    sig_ref,
    sub_ref,
    left,
    right,
    v1,
    v2,
    acc,
    rs_core,
    rs_send,
    rs_recv,
    ar1,
    ar2,
    ar3,
    keep,
    send,
    recv,
    local_sem,
):
    term = lax.axis_index("term")
    sector = lax.axis_index("sector")
    c = term % NC
    x = (term // NC) % NX
    zh = term // (NX * NC)
    y = sector // NZL
    zl = sector % NZL
    z = zh * NZL + zl
    terms = left.shape[0]
    me = (x, y, z, c)

    def at(dx=0, dy=0, dz=0, dc=0):
        return device((x + dx) % NX, (y + dy) % NY, (z + dz) % NZ, (c + dc) % NC)

    def copy(src, dst, slot, dev):
        return pltpu.make_async_remote_copy(
            src_ref=src,
            dst_ref=dst,
            send_sem=send.at[slot],
            recv_sem=recv.at[slot],
            device_id=dev,
            device_id_type=MESH,
        )

    load_left = pltpu.make_async_copy(left_hbm.at[:, 0], left, local_sem.at[0])
    load_right = pltpu.make_async_copy(right_hbm.at[:, 0], right, local_sem.at[1])
    load_left.start()
    load_right.start()

    rows = term * 16 + lax.broadcasted_iota(jnp.int32, (16, 512), 0)
    cols = lax.broadcasted_iota(jnp.int32, (16, 512), 1)
    size = bs_ref[sector]
    valid = ((rows < size) & (cols < size)).astype(F32)
    masked = wave_ref[0] * valid
    keep[0] = masked
    v1[y, zl, zh, x, c] = masked.astype(BF16)

    barrier = pltpu.get_barrier_semaphore()
    peers = [at(dx=d) for d in (1, 2, 3)] + [at(dy=d) for d in (1, 2, 3)]
    peers += [at(dz=d) for d in (1, 7)] + [at(dc=1)]
    for dev in peers:
        pl.semaphore_signal(barrier, inc=1, device_id=dev, device_id_type=MESH)
    pl.semaphore_wait(barrier, len(peers))

    def gather(v, cs):
        if cs == 0:
            f, g = x, y

            def ref(gg, zz, ff):
                return v.at[gg, zz % NZL, zz // NZL, ff, 0]

            def dev_f(d):
                return at(dx=d)

            def dev_g(d):
                return at(dy=d)

        else:
            f, g = y, x

            def ref(gg, zz, ff):
                return v.at[ff, zz % NZL, zz // NZL, gg, 1]

            def dev_f(d):
                return at(dy=d)

            def dev_g(d):
                return at(dx=d)

        every, half_a, half_b = slice(None), pl.ds(0, 2), pl.ds(2, 2)
        sent = []
        mirrored = []

        def go(slot, gg, zz, ff, dev):
            cp = copy(ref(gg, zz, ff), ref(gg, zz, ff), slot, dev)
            cp.start()
            sent.append(cp)

        def got(slot, gg, zz, ff):
            copy(ref(gg, zz, ff), ref(gg, zz, ff), slot, at(dc=1)).wait_recv()

        def mirror(gg, zz):
            slot = AG_M + len(mirrored)
            mirrored.append((gg, zz))
            go(slot, gg, zz, every, at(dc=1))

        gi = lambda d: (g + d) % 4
        fi = lambda d: (f + d) % 4
        zi = lambda d: (z + d) % NZ

        for d in (2, 1, 3):
            go(AG_FIRST + d - 1, g, z, f, dev_f(d))
        for d in (1, 3, 2):
            got(AG_FIRST + d - 1, g, z, fi(-d))

        def g_send(b):
            zz = zi(b)
            go(AG_GR + b % 8, g, zz, every, dev_g(1))
            go(AG_GL + b % 8, g, zz, every, dev_g(-1))
            mirror(g, zz)

        def g_pass(b):
            zz = zi(b)
            got(AG_GR + b % 8, gi(-1), zz, every)
            go(AG_HR + b % 8, gi(-1), zz, half_a, dev_g(1))
            mirror(gi(-1), zz)
            got(AG_GL + b % 8, gi(1), zz, every)
            go(AG_HL + b % 8, gi(1), zz, half_b, dev_g(-1))
            mirror(gi(1), zz)

        def g_end(b):
            zz = zi(b)
            got(AG_HR + b % 8, gi(2), zz, half_a)
            got(AG_HL + b % 8, gi(2), zz, half_b)
            mirror(gi(2), zz)

        go(AG_ZR, g, z, every, at(dz=1))
        go(AG_ZL, g, z, every, at(dz=-1))
        g_send(0)
        for k in (1, 2, 3):
            got(AG_ZR + k - 1, g, zi(-k), every)
            go(AG_ZR + k, g, zi(-k), every if k < 3 else half_a, at(dz=1))
            got(AG_ZL + k - 1, g, zi(k), every)
            go(AG_ZL + k, g, zi(k), every if k < 3 else half_b, at(dz=-1))
            g_send(-k)
            g_send(k)
            if k == 1:
                g_pass(0)
            else:
                g_pass(1 - k)
                g_pass(k - 1)
        got(AG_ZR + 3, g, zi(4), half_a)
        got(AG_ZL + 3, g, zi(4), half_b)
        g_send(4)
        g_pass(-3)
        g_pass(3)
        for b in (0, -1, 1):
            g_end(b)
        g_pass(4)
        for b in (-2, 2, -3, 3, 4):
            g_end(b)
        for i in range(len(mirrored)):
            slot = AG_M + i
            copy(ref(g, z, every), ref(g, z, every), slot, at(dc=1)).wait_recv()
        for cp in sent:
            cp.wait_send()

    def all_gather(v):
        @pl.when(c == 0)
        def _():
            gather(v, 0)

        @pl.when(c == 1)
        def _():
            gather(v, 1)

    def apply_ops(v):
        acc[...] = jnp.zeros_like(acc)

        def step(t, carry):
            src = source_ref[t, sector]
            block = v[src >> 1, src & 1].reshape(512, 512)
            half = jnp.dot(left[t], block, preferred_element_type=F32).astype(BF16)
            part = lax.dot_general(
                half, right[t], (((1,), (1,)), ((), ())), preferred_element_type=F32
            )
            acc[...] += part.reshape(acc.shape)
            return carry

        lax.fori_loop(0, terms, step, 0)

    def row(p):
        p = jnp.sum(p.reshape(-1, 8, 512), axis=0)
        p = p[:, :128] + p[:, 128:256] + p[:, 256:384] + p[:, 384:]
        return jnp.sum(p, axis=0, keepdims=True)

    def inner(v):
        def step(i, carry):
            prod = v[y, zl, i].astype(F32) * acc[i]
            return carry + jnp.sum(prod.reshape(-1, 8, 512), axis=0)

        return row(lax.fori_loop(0, NZH, step, jnp.zeros((8, 512), F32)))

    def tile(parts):
        index = lax.broadcasted_iota(jnp.int32, (8, 128), 0)
        out = jnp.zeros((8, 128), F32)
        for i, p in enumerate(parts):
            out = jnp.where(index == i, jnp.broadcast_to(p, (8, 128)), out)
        return out

    def reduce_out(parts_of):
        core = copy(acc.at[:, :, 1 - c], rs_core, RS_C, at(dc=1))
        core.start()
        sent = [core]
        mine1 = x * NC + c
        ar1[mine1] = tile(parts_of())
        for d in range(1, 8):
            k = (mine1 + d) % 8
            dev = device(k // NC, y, z, k % NC)
            cp = copy(ar1.at[mine1], ar1.at[mine1], AR1 + d, dev)
            cp.start()
            sent.append(cp)
        core.wait_recv()
        rs_core[...] = acc[:, :, c] + rs_core[...]
        rs_send[...] = rs_core[...].astype(BF16)
        mine = zh * NX + x
        for dzh in (2, 1, 3, 0):
            for dx in (2, 1, 3, 0):
                if dzh == 0 and dx == 0:
                    continue
                slot = dzh * NX + dx
                zt = (zh + dzh) % NZH
                xt = (x + dx) % NX
                cp = copy(
                    rs_send.at[zt, xt],
                    rs_recv.at[slot],
                    RS + slot,
                    device(xt, y, zt * NZL + zl, c),
                )
                cp.start()
                sent.append(cp)
        for d in range(1, 8):
            k = (mine1 + 8 - d) % 8
            copy(ar1.at[k], ar1.at[k], AR1 + d, at(dc=1)).wait_recv()
        ar2[y] = jnp.sum(ar1[...], axis=0)
        for d in (2, 1, 3):
            cp = copy(ar2.at[y], ar2.at[y], AR2 + d, at(dy=d))
            cp.start()
            sent.append(cp)
        for d in (1, 3, 2):
            k = (y + 4 - d) % 4
            copy(ar2.at[k], ar2.at[k], AR2 + d, at(dc=1)).wait_recv()
        ar3[z] = jnp.sum(ar2[...], axis=0)
        for d in (4, 3, 5, 2, 6, 1, 7):
            cp = copy(ar3.at[z], ar3.at[z], AR3 + d, at(dz=d))
            cp.start()
            sent.append(cp)
        result = rs_core[zh, x]
        for dzh in (0, 1, 3, 2):
            for dx in (0, 1, 3, 2):
                slot = dzh * NX + dx
                if slot == 0:
                    continue
                copy(rs_recv.at[slot], rs_recv.at[slot], RS + slot, at(dc=1)).wait_recv()
                result = result + rs_recv[slot].astype(F32)
        for d in range(1, 8):
            k = (z + 8 - d) % 8
            copy(ar3.at[k], ar3.at[k], AR3 + d, at(dc=1)).wait_recv()
        sums = jnp.sum(ar3[...], axis=0)
        for cp in sent:
            cp.wait_send()
        return result * valid, sums

    def scalar(sums, i):
        return jnp.sum(sums[i : i + 1, :], axis=1, keepdims=True)

    all_gather(v1)
    load_left.wait()
    load_right.wait()
    apply_ops(v1)
    raw, sums = reduce_out(lambda: [row(keep[0] * keep[0]), inner(v1)])
    squares = scalar(sums, 0) / total
    scale = 1.0 / jnp.sqrt(squares + 1e-06)
    theta = scale * scale * scalar(sums, 1) / total
    first_vec = keep[0] * scale
    first_sigma = raw * scale
    correction = (first_sigma - theta * first_vec) / jnp.maximum(
        jnp.abs(diag_ref[0] - theta), 1.0
    )
    keep[1] = correction
    keep[2] = first_sigma
    keep[0] = first_vec
    v2[y, zl, zh, x, c] = correction.astype(BF16)

    all_gather(v2)
    apply_ops(v2)
    raw2, sums = reduce_out(
        lambda: [
            row(keep[0] * keep[1]),
            row(keep[1] * keep[1]),
            row(keep[1] * keep[2]),
            inner(v1) * scale,
            inner(v2),
        ]
    )
    first_sq = scale * scale * squares
    corre = scalar(sums, 0) / total
    corr_sq = scalar(sums, 1) / total
    corr_sigma = scalar(sums, 2) / total
    first_raw = scalar(sums, 3) / total
    corr_raw = scalar(sums, 4) / total
    orth_sq = jnp.maximum(corr_sq - 2.0 * corre * corre + corre * corre * first_sq, 0.0)
    norm = 1.0 / jnp.sqrt(orth_sq + 1e-06)
    vec_ref[0] = (keep[1] - corre * keep[0]) * norm
    sig_ref[0] = (raw2 - corre * keep[2]) * norm
    upper = (first_raw - corre * theta) * norm
    lower = (corr_sigma - corre * theta) * norm
    corner = (
        (corr_raw - corre * corr_sigma - corre * first_raw + corre * corre * theta)
        * norm
        * norm
    )
    r = lax.broadcasted_iota(jnp.int32, (2, 2), 0)
    q = lax.broadcasted_iota(jnp.int32, (2, 2), 1)
    low = jnp.where(q == 0, lower, corner)
    high = jnp.where(q == 0, theta, upper)
    sub_ref[...] = jnp.where(r == 0, high, low)


def local(wave, left_ops, right_ops, diagonal, block_size, source):
    terms, _, width, _ = left_ops.shape
    total = float(block_size.shape[0] * width * width)
    vmem = pl.BlockSpec(memory_space=pltpu.VMEM)
    smem = pl.BlockSpec(memory_space=pltpu.SMEM)
    hbm = pl.BlockSpec(memory_space=pl.ANY)
    slab = (16, width)

    def body(*refs):
        kernel(total, *refs)

    return pl.pallas_call(
        body,
        out_shape=(
            jax.ShapeDtypeStruct((1,) + slab, F32),
            jax.ShapeDtypeStruct((1,) + slab, F32),
            jax.ShapeDtypeStruct((2, 2), F32),
        ),
        in_specs=[smem, smem, vmem, vmem, hbm, hbm],
        out_specs=(vmem, vmem, vmem),
        scratch_shapes=[
            pltpu.VMEM((terms, width, width), BF16),
            pltpu.VMEM((terms, width, width), BF16),
            pltpu.VMEM((NY, NZL, NZH, NX, NC) + slab, BF16),
            pltpu.VMEM((NY, NZL, NZH, NX, NC) + slab, BF16),
            pltpu.VMEM((NZH, NX, NC) + slab, F32),
            pltpu.VMEM((NZH, NX) + slab, F32),
            pltpu.VMEM((NZH, NX) + slab, BF16),
            pltpu.VMEM((NZH * NX,) + slab, BF16),
            pltpu.VMEM((8, 8, 128), F32),
            pltpu.VMEM((4, 8, 128), F32),
            pltpu.VMEM((8, 8, 128), F32),
            pltpu.VMEM((3,) + slab, F32),
            pltpu.SemaphoreType.DMA((NSEM,)),
            pltpu.SemaphoreType.DMA((NSEM,)),
            pltpu.SemaphoreType.DMA((2,)),
        ],
        compiler_params=pltpu.CompilerParams(
            collective_id=0, has_side_effects=True, vmem_limit_bytes=48 * 1024 * 1024
        ),
    )(block_size, source, wave, diagonal, left_ops, right_ops)


def solution(mesh):
    return jax.shard_map(
        local,
        mesh=mesh,
        in_specs=(
            P("sector", "term", None),
            P("term", "sector", None, None),
            P("term", "sector", None, None),
            P("sector", "term", None),
            P(),
            P("term", None),
        ),
        out_specs=(P("sector", "term", None), P("sector", "term", None), P()),
        check_vma=False,
    )
```

```python
import jax
import jax.numpy as jnp
from jax import lax
from jax.experimental import pallas as pl
from jax.experimental.pallas import tpu as pltpu
from jax.sharding import PartitionSpec as P

MESH = pl.DeviceIdType.MESH
F32 = jnp.float32
BF16 = jnp.bfloat16

NX, NY, NZH, NZL, NC = 4, 4, 4, 2, 2
NZ = NZH * NZL

TERMS_AT_ONCE = 2

AG_F2 = 0
AG_Z = 1
AG_Z2 = 8
AG_F = 15
AG_GR = 17
AG_GL = 21
AG_HR = 25
AG_HL = 29
AG_M = 33
RS_C = 49
RS = 50
AR1 = 66
AR2 = 82
NSEM = 98


def kernel(
    total,
    bs_hbm,
    source_hbm,
    wave_hbm,
    diag_hbm,
    left_hbm,
    right_hbm,
    vec_ref,
    sig_ref,
    sub_ref,
    bs_ref,
    source_ref,
    wave_ref,
    diag_ref,
    left,
    right,
    v1,
    v2,
    acc,
    rs_core,
    rs_send,
    rs_recv,
    ar1,
    ar2,
    keep,
    send,
    recv,
    local_sem,
):
    term = lax.axis_index("term")
    sector = lax.axis_index("sector")
    c = term % NC
    x = (term // NC) % NX
    zh = term // (NX * NC)
    y = sector // NZL
    zl = sector % NZL
    z = zh * NZL + zl
    terms = left.shape[0]

    xs = [x] + [(x + d) % NX for d in range(1, NX)]
    ys = [y] + [(y + d) % NY for d in range(1, NY)]
    zs = [z] + [(z + d) % NZ for d in range(1, NZ)]
    zhs = [zh] + [zz // NZL for zz in zs[1:]]
    zls = [zl, 1 - zl] * NZH
    cs_ = [c, 1 - c]

    def at(dx=0, dy=0, dz=0, dc=0):
        dx, dy, dz = dx % NX, dy % NY, dz % NZ
        return {
            "term": zhs[dz] * (NX * NC) + xs[dx] * NC + cs_[dc],
            "sector": ys[dy] * NZL + zls[dz],
        }

    def copy(src, dst, slot, dev):
        return pltpu.make_async_remote_copy(
            src_ref=src,
            dst_ref=dst,
            send_sem=send.at[slot],
            recv_sem=recv.at[slot],
            device_id=dev,
            device_id_type=MESH,
        )

    def load(src, dst, i):
        cp = pltpu.make_async_copy(src, dst, local_sem.at[i])
        cp.start()
        return cp

    barrier = pltpu.get_barrier_semaphore()
    peers = [at(dx=d) for d in (1, 2, 3)] + [at(dy=d) for d in (1, 2, 3)]
    peers += [at(dz=d) for d in range(1, NZ)] + [at(dc=1)]
    for dev in peers:
        pl.semaphore_signal(barrier, inc=1, device_id=dev, device_id_type=MESH)
    load_wave = load(wave_hbm, wave_ref, 0)
    load_bs = load(bs_hbm, bs_ref, 1)
    load_source = load(source_hbm, source_ref, 2)
    load_diag = load(diag_hbm, diag_ref, 3)
    load_left = load(left_hbm.at[:, 0], left, 4)
    load_right = load(right_hbm.at[:, 0], right, 5)

    load_bs.wait()
    load_wave.wait()
    rows = term * 16 + lax.broadcasted_iota(jnp.int32, (16, 512), 0)
    cols = lax.broadcasted_iota(jnp.int32, (16, 512), 1)
    size = bs_ref[sector]
    valid = ((rows < size) & (cols < size)).astype(F32)
    masked = wave_ref[0] * valid
    keep[0] = masked
    v1[y, zl, zh, x, c] = masked.astype(BF16)
    pl.semaphore_wait(barrier, len(peers))

    def gather(v, cs):
        fs, gs = (xs, ys) if cs == 0 else (ys, xs)
        every = slice(None)
        sent = []

        def piece(df, dz):
            i, j = (gs[0], fs[df % 4]) if cs == 0 else (fs[df % 4], gs[0])
            return v.at[i, zls[dz % NZ], zhs[dz % NZ], j, cs]

        def block(df, dg, part=every):
            i, j = (gs[dg % 4], fs[df % 4]) if cs == 0 else (fs[df % 4], gs[dg % 4])
            return v.at[i, :, part, j, cs]

        half_a, half_b = pl.ds(0, 2), pl.ds(2, 2)

        def dev_f(d):
            return at(dx=d) if cs == 0 else at(dy=d)

        def dev_g(d):
            return at(dy=d) if cs == 0 else at(dx=d)

        def go(slot, of, dev):
            copy(of(), of(), slot, dev).start()
            sent.append((slot, of))

        def got(slot, of):
            copy(of(), of(), slot, at(dc=1)).wait_recv()

        def mirror(df, dg):
            of = lambda: block(df, dg)
            go(AG_M + (df % 4) * 4 + dg % 4, of, at(dc=1))

        def g_send(df):
            go(AG_GR + df % 4, lambda: block(df, 0), dev_g(1))
            go(AG_GL + df % 4, lambda: block(df, 0), dev_g(-1))
            mirror(df, 0)

        def g_pass(df):
            got(AG_GR + df % 4, lambda: block(df, -1))
            go(AG_HR + df % 4, lambda: block(df, -1, half_a), dev_g(1))
            mirror(df, -1)
            got(AG_GL + df % 4, lambda: block(df, 1))
            go(AG_HL + df % 4, lambda: block(df, 1, half_b), dev_g(-1))
            mirror(df, 1)

        def g_end(df):
            got(AG_HR + df % 4, lambda: block(df, 2, half_a))
            got(AG_HL + df % 4, lambda: block(df, 2, half_b))
            mirror(df, 2)

        def z_send(df, slot):
            for d in (4, 3, 5, 2, 6, 1, 7):
                go(slot + d - 1, lambda: piece(df, 0), at(dz=d))

        def z_got(df, slot):
            for d in (1, 7, 2, 6, 3, 5, 4):
                got(slot + d - 1, lambda: piece(df, -d))

        def first():
            go(AG_F2, lambda: piece(0, 0), dev_f(2))
            z_send(0, AG_Z)

        def second():
            got(AG_F2, lambda: piece(2, 0))
            z_send(2, AG_Z2)

        def third():
            z_got(0, AG_Z)
            go(AG_F, lambda: block(0, 0), dev_f(1))
            go(AG_F + 1, lambda: block(0, 0), dev_f(-1))
            g_send(0)

        def fourth():
            z_got(2, AG_Z2)
            g_send(2)

        def fifth():
            got(AG_F, lambda: block(-1, 0))
            g_send(-1)
            got(AG_F + 1, lambda: block(1, 0))
            g_send(1)

        def pass_0():
            g_pass(0)

        def pass_2():
            g_pass(2)

        def pass_1():
            g_pass(-1)
            g_pass(1)

        def end_0():
            g_end(0)

        def end_2():
            g_end(2)

        def end_1():
            g_end(-1)
            g_end(1)

        def last():
            for i in range(16):
                got(AG_M + i, lambda: block(0, 0))

        def sent_all():
            for slot, of in sent:
                copy(of(), of(), slot, at(dc=1)).wait_send()

        arrive = [first, third, second, pass_0, fifth, fourth]
        arrive += [end_0, pass_1, pass_2, end_1, end_2, last]
        return arrive, sent_all

    def all_gather(v):
        steps = [gather(v, cs) for cs in range(NC)]

        def run(todo):
            for cs in range(NC):

                @pl.when(c == cs)
                def _(cs=cs):
                    for step in todo(*steps[cs]):
                        step()

        run(lambda arrive, sent_all: arrive)
        return lambda: run(lambda arrive, sent_all: [sent_all])

    def apply_ops(v):
        acc[...] = jnp.zeros_like(acc)

        def step(i, carry):
            halves, rights = [], []
            for k in range(TERMS_AT_ONCE):
                t = i * TERMS_AT_ONCE + k
                src = source_ref[t, sector]
                block = v[src >> 1, src & 1].reshape(512, 512)
                half = jnp.dot(left[t], block, preferred_element_type=F32)
                halves.append(half.astype(BF16))
                rights.append(right[t])
            part = lax.dot_general(
                jnp.concatenate(halves, axis=1),
                jnp.concatenate(rights, axis=1),
                (((1,), (1,)), ((), ())),
                preferred_element_type=F32,
            )
            acc[...] += part.reshape(acc.shape)
            return carry

        lax.fori_loop(0, terms // TERMS_AT_ONCE, step, 0)

    def row(p):
        p = jnp.sum(p.reshape(-1, 8, 512), axis=0)
        p = p[:, :128] + p[:, 128:256] + p[:, 256:384] + p[:, 384:]
        return jnp.sum(p, axis=0, keepdims=True)

    def inner(v):
        def step(i, carry):
            prod = v[y, zl, i].astype(F32) * acc[i]
            return carry + jnp.sum(prod.reshape(-1, 8, 512), axis=0)

        return row(lax.fori_loop(0, NZH, step, jnp.zeros((8, 512), F32)))

    def tile(parts):
        index = lax.broadcasted_iota(jnp.int32, (8, 128), 0)
        out = jnp.zeros((8, 128), F32)
        for i, p in enumerate(parts):
            out = jnp.where(index == i, jnp.broadcast_to(p, (8, 128)), out)
        return out

    def reduce_out(parts_of, left_to_wait):
        core = copy(acc.at[:, :, 1 - c], rs_core, RS_C, at(dc=1))
        core.start()
        sent = [core]
        ar1[z, c] = tile(parts_of())
        far = (4, 3, 5, 2, 6, 1, 7, 0)
        zc = [(dz, dc) for dz in far for dc in (0, 1) if dz or dc]
        xy = [(dx, dy) for dx in (2, 1, 3, 0) for dy in (2, 1, 3, 0) if dx or dy]
        for dz, dc in zc:
            cp = copy(ar1.at[z, c], ar1.at[z, c], AR1 + dz * NC + dc, at(dz=dz, dc=dc))
            cp.start()
            sent.append(cp)
        core.wait_recv()
        rs_core[...] = acc[:, :, c] + rs_core[...]
        rs_send[...] = rs_core[...].astype(BF16)
        zx = [(dzh, dx) for dzh in (2, 1, 3, 0) for dx in (2, 1, 3, 0) if dzh or dx]
        for dzh, dx in zx:
            slot = dzh * NX + dx
            cp = copy(
                rs_send.at[zhs[dzh * NZL], xs[dx]],
                rs_recv.at[slot],
                RS + slot,
                at(dx=dx, dz=dzh * NZL),
            )
            cp.start()
            sent.append(cp)
        for dz, dc in reversed(zc):
            other = ar1.at[zs[-dz % NZ], cs_[dc]]
            copy(other, other, AR1 + dz * NC + dc, at(dc=1)).wait_recv()
        ar2[x, y] = jnp.sum(ar1[...].reshape(NZ * NC, 8, 128), axis=0)
        for dx, dy in xy:
            cp = copy(ar2.at[x, y], ar2.at[x, y], AR2 + dx * NY + dy, at(dx=dx, dy=dy))
            cp.start()
            sent.append(cp)
        left_to_wait()
        result = rs_core[zh, x]
        for dzh, dx in reversed(zx):
            slot = dzh * NX + dx
            copy(rs_recv.at[slot], rs_recv.at[slot], RS + slot, at(dc=1)).wait_recv()
            result = result + rs_recv[slot].astype(F32)
        for dx, dy in reversed(xy):
            other = ar2.at[xs[-dx % NX], ys[-dy % NY]]
            copy(other, other, AR2 + dx * NY + dy, at(dc=1)).wait_recv()
        sums = jnp.sum(ar2[...].reshape(NX * NY, 8, 128), axis=0)

        def finish():
            for cp in sent:
                cp.wait_send()

        return result * valid, sums, finish

    def scalar(sums, i):
        return jnp.sum(sums[i : i + 1, :], axis=1, keepdims=True)

    left_to_wait = all_gather(v1)
    load_source.wait()
    load_left.wait()
    load_right.wait()
    apply_ops(v1)
    raw, sums, finish = reduce_out(
        lambda: [row(keep[0] * keep[0]), inner(v1)], left_to_wait
    )
    load_diag.wait()
    squares = scalar(sums, 0) / total
    scale = 1.0 / jnp.sqrt(squares + 1e-06)
    theta = scale * scale * scalar(sums, 1) / total
    first_vec = keep[0] * scale
    first_sigma = raw * scale
    correction = (first_sigma - theta * first_vec) / jnp.maximum(
        jnp.abs(diag_ref[0] - theta), 1.0
    )
    keep[1] = correction
    keep[2] = first_sigma
    keep[0] = first_vec
    v2[y, zl, zh, x, c] = correction.astype(BF16)

    left_to_wait = all_gather(v2)
    finish()
    apply_ops(v2)
    raw2, sums, finish = reduce_out(
        lambda: [
            row(keep[0] * keep[1]),
            row(keep[1] * keep[1]),
            row(keep[1] * keep[2]),
            inner(v1) * scale,
            inner(v2),
        ],
        left_to_wait,
    )
    first_sq = scale * scale * squares
    corre = scalar(sums, 0) / total
    corr_sq = scalar(sums, 1) / total
    corr_sigma = scalar(sums, 2) / total
    first_raw = scalar(sums, 3) / total
    corr_raw = scalar(sums, 4) / total
    orth_sq = jnp.maximum(corr_sq - 2.0 * corre * corre + corre * corre * first_sq, 0.0)
    norm = 1.0 / jnp.sqrt(orth_sq + 1e-06)
    vec_ref[0] = (keep[1] - corre * keep[0]) * norm
    sig_ref[0] = (raw2 - corre * keep[2]) * norm
    upper = (first_raw - corre * theta) * norm
    lower = (corr_sigma - corre * theta) * norm
    corner = (
        (corr_raw - corre * corr_sigma - corre * first_raw + corre * corre * theta)
        * norm
        * norm
    )
    r = lax.broadcasted_iota(jnp.int32, (2, 2), 0)
    q = lax.broadcasted_iota(jnp.int32, (2, 2), 1)
    low = jnp.where(q == 0, lower, corner)
    high = jnp.where(q == 0, theta, upper)
    sub_ref[...] = jnp.where(r == 0, high, low)
    finish()


def local(wave, left_ops, right_ops, diagonal, block_size, source):
    terms, _, width, _ = left_ops.shape
    total = float(block_size.shape[0] * width * width)
    vmem = pl.BlockSpec(memory_space=pltpu.VMEM)
    hbm = pl.BlockSpec(memory_space=pltpu.HBM)
    slab = (16, width)

    def body(*refs):
        kernel(total, *refs)

    return pl.pallas_call(
        body,
        out_shape=(
            jax.ShapeDtypeStruct((1,) + slab, F32),
            jax.ShapeDtypeStruct((1,) + slab, F32),
            jax.ShapeDtypeStruct((2, 2), F32),
        ),
        in_specs=[hbm] * 6,
        out_specs=(vmem, vmem, vmem),
        scratch_shapes=[
            pltpu.SMEM(block_size.shape, jnp.int32),
            pltpu.SMEM(source.shape, jnp.int32),
            pltpu.VMEM((1,) + slab, F32),
            pltpu.VMEM((1,) + slab, F32),
            pltpu.VMEM((terms, width, width), BF16),
            pltpu.VMEM((terms, width, width), BF16),
            pltpu.VMEM((NY, NZL, NZH, NX, NC) + slab, BF16),
            pltpu.VMEM((NY, NZL, NZH, NX, NC) + slab, BF16),
            pltpu.VMEM((NZH, NX, NC) + slab, F32),
            pltpu.VMEM((NZH, NX) + slab, F32),
            pltpu.VMEM((NZH, NX) + slab, BF16),
            pltpu.VMEM((NZH * NX,) + slab, BF16),
            pltpu.VMEM((NZ, NC, 8, 128), F32),
            pltpu.VMEM((NX, NY, 8, 128), F32),
            pltpu.VMEM((3,) + slab, F32),
            pltpu.SemaphoreType.DMA((NSEM,)),
            pltpu.SemaphoreType.DMA((NSEM,)),
            pltpu.SemaphoreType.DMA((6,)),
        ],
        compiler_params=pltpu.CompilerParams(
            collective_id=0, has_side_effects=True, vmem_limit_bytes=60 * 1024 * 1024
        ),
    )(block_size, source, wave, diagonal, left_ops, right_ops)


def solution(mesh):
    return jax.shard_map(
        local,
        mesh=mesh,
        in_specs=(
            P("sector", "term", None),
            P("term", "sector", None, None),
            P("term", "sector", None, None),
            P("sector", "term", None),
            P(),
            P("term", None),
        ),
        out_specs=(P("sector", "term", None), P("sector", "term", None), P()),
        check_vma=False,
    )
```

```python
import jax
import jax.numpy as jnp
from jax import lax
from jax.experimental import pallas as pl
from jax.experimental.pallas import tpu as pltpu
from jax.sharding import PartitionSpec as P

MESH = pl.DeviceIdType.MESH
F32 = jnp.float32
BF16 = jnp.bfloat16

NX, NY, NZH, NZL, NC = 4, 4, 4, 2, 2
NZ = NZH * NZL

TERMS_AT_ONCE = 4

AG_F2 = 0
AG_Z = 1
AG_Z2 = 8
AG_F = 15
AG_GR = 17
AG_GL = 21
AG_HR = 25
AG_HL = 29
AG_M = 33
RS_C = 49
RS = 50
AR1 = 66
AR2 = 82
NSEM = 98


def kernel(
    total,
    bs_hbm,
    source_hbm,
    wave_hbm,
    diag_hbm,
    left_hbm,
    right_hbm,
    vec_ref,
    sig_ref,
    sub_ref,
    bs_ref,
    source_ref,
    wave_ref,
    diag_ref,
    left,
    right,
    v1,
    v2,
    acc,
    rs_core,
    rs_send,
    rs_recv,
    ar1,
    ar2,
    keep,
    send,
    recv,
    local_sem,
):
    term = lax.axis_index("term")
    sector = lax.axis_index("sector")
    c = term % NC
    x = (term // NC) % NX
    zh = term // (NX * NC)
    y = sector // NZL
    zl = sector % NZL
    z = zh * NZL + zl
    terms = left.shape[0]

    xs = [x] + [(x + d) % NX for d in range(1, NX)]
    ys = [y] + [(y + d) % NY for d in range(1, NY)]
    zs = [z] + [(z + d) % NZ for d in range(1, NZ)]
    zhs = [zh] + [zz // NZL for zz in zs[1:]]
    zls = [zl, 1 - zl] * NZH
    cs_ = [c, 1 - c]

    def at(dx=0, dy=0, dz=0, dc=0):
        dx, dy, dz = dx % NX, dy % NY, dz % NZ
        return {
            "term": zhs[dz] * (NX * NC) + xs[dx] * NC + cs_[dc],
            "sector": ys[dy] * NZL + zls[dz],
        }

    def copy(src, dst, slot, dev):
        return pltpu.make_async_remote_copy(
            src_ref=src,
            dst_ref=dst,
            send_sem=send.at[slot],
            recv_sem=recv.at[slot],
            device_id=dev,
            device_id_type=MESH,
        )

    def load(src, dst, i):
        cp = pltpu.make_async_copy(src, dst, local_sem.at[i])
        cp.start()
        return cp

    barrier = pltpu.get_barrier_semaphore()
    peers = [at(dx=d) for d in (1, 2, 3)] + [at(dy=d) for d in (1, 2, 3)]
    peers += [at(dz=d) for d in range(1, NZ)] + [at(dc=1)]
    for dev in peers:
        pl.semaphore_signal(barrier, inc=1, device_id=dev, device_id_type=MESH)
    load_wave = load(wave_hbm, wave_ref, 0)
    load_bs = load(bs_hbm, bs_ref, 1)
    load_source = load(source_hbm, source_ref, 2)
    load_diag = load(diag_hbm, diag_ref, 3)
    load_left = load(left_hbm.at[:, 0], left, 4)
    load_right = load(right_hbm.at[:, 0], right, 5)

    load_bs.wait()
    load_wave.wait()
    rows = term * 16 + lax.broadcasted_iota(jnp.int32, (16, 512), 0)
    cols = lax.broadcasted_iota(jnp.int32, (16, 512), 1)
    size = bs_ref[sector]
    valid = ((rows < size) & (cols < size)).astype(F32)
    masked = wave_ref[0] * valid
    keep[0] = masked
    v1[y, zl, zh, x, c] = masked.astype(BF16)
    pl.semaphore_wait(barrier, len(peers))

    def gather(v, cs):
        fs, gs = (xs, ys) if cs == 0 else (ys, xs)
        every = slice(None)
        sent = []

        def piece(df, dz):
            i, j = (gs[0], fs[df % 4]) if cs == 0 else (fs[df % 4], gs[0])
            return v.at[i, zls[dz % NZ], zhs[dz % NZ], j, cs]

        def block(df, dg, part=every):
            i, j = (gs[dg % 4], fs[df % 4]) if cs == 0 else (fs[df % 4], gs[dg % 4])
            return v.at[i, :, part, j, cs]

        half_a, half_b = pl.ds(0, 2), pl.ds(2, 2)

        def dev_f(d):
            return at(dx=d) if cs == 0 else at(dy=d)

        def dev_g(d):
            return at(dy=d) if cs == 0 else at(dx=d)

        def go(slot, of, dev):
            copy(of(), of(), slot, dev).start()
            sent.append((slot, of))

        def got(slot, of):
            copy(of(), of(), slot, at(dc=1)).wait_recv()

        def mirror(df, dg):
            of = lambda: block(df, dg)
            go(AG_M + (df % 4) * 4 + dg % 4, of, at(dc=1))

        def g_send(df):
            go(AG_GR + df % 4, lambda: block(df, 0), dev_g(1))
            go(AG_GL + df % 4, lambda: block(df, 0), dev_g(-1))
            mirror(df, 0)

        def g_pass(df):
            got(AG_GR + df % 4, lambda: block(df, -1))
            go(AG_HR + df % 4, lambda: block(df, -1, half_a), dev_g(1))
            mirror(df, -1)
            got(AG_GL + df % 4, lambda: block(df, 1))
            go(AG_HL + df % 4, lambda: block(df, 1, half_b), dev_g(-1))
            mirror(df, 1)

        def g_end(df):
            got(AG_HR + df % 4, lambda: block(df, 2, half_a))
            got(AG_HL + df % 4, lambda: block(df, 2, half_b))
            mirror(df, 2)

        def z_send(df, slot):
            for d in (4, 3, 5, 2, 6, 1, 7):
                go(slot + d - 1, lambda: piece(df, 0), at(dz=d))

        def z_got(df, slot):
            for d in (1, 7, 2, 6, 3, 5, 4):
                got(slot + d - 1, lambda: piece(df, -d))

        def first():
            go(AG_F2, lambda: piece(0, 0), dev_f(2))
            z_send(0, AG_Z)

        def second():
            got(AG_F2, lambda: piece(2, 0))
            z_send(2, AG_Z2)

        def third():
            z_got(0, AG_Z)
            go(AG_F, lambda: block(0, 0), dev_f(1))
            go(AG_F + 1, lambda: block(0, 0), dev_f(-1))
            g_send(0)

        def fourth():
            z_got(2, AG_Z2)
            g_send(2)

        def fifth():
            got(AG_F, lambda: block(-1, 0))
            g_send(-1)
            got(AG_F + 1, lambda: block(1, 0))
            g_send(1)

        def pass_0():
            g_pass(0)

        def pass_2():
            g_pass(2)

        def pass_1():
            g_pass(-1)
            g_pass(1)

        def end_0():
            g_end(0)

        def end_2():
            g_end(2)

        def end_1():
            g_end(-1)
            g_end(1)

        def last():
            for i in range(16):
                got(AG_M + i, lambda: block(0, 0))

        def sent_all():
            for slot, of in sent:
                copy(of(), of(), slot, at(dc=1)).wait_send()

        arrive = [first, third, second, pass_0, fifth, fourth]
        arrive += [end_0, pass_1, pass_2, end_1, end_2, last]
        return arrive, sent_all

    def all_gather(v):
        steps = [gather(v, cs) for cs in range(NC)]

        def run(todo):
            for cs in range(NC):

                @pl.when(c == cs)
                def _(cs=cs):
                    for step in todo(*steps[cs]):
                        step()

        run(lambda arrive, sent_all: arrive)
        return lambda: run(lambda arrive, sent_all: [sent_all])

    def apply_ops(v):
        acc[...] = jnp.zeros_like(acc)

        def step(i, carry):
            halves, rights = [], []
            for k in range(TERMS_AT_ONCE):
                t = i * TERMS_AT_ONCE + k
                src = source_ref[t, sector]
                block = v[src >> 1, src & 1].reshape(512, 512)
                half = jnp.dot(left[t], block, preferred_element_type=F32)
                halves.append(half.astype(BF16))
                rights.append(right[t])
            part = lax.dot_general(
                jnp.concatenate(halves, axis=1),
                jnp.concatenate(rights, axis=1),
                (((1,), (1,)), ((), ())),
                preferred_element_type=F32,
            )
            acc[...] += part.reshape(acc.shape)
            return carry

        lax.fori_loop(0, terms // TERMS_AT_ONCE, step, 0)

    def row(p):
        p = jnp.sum(p.reshape(-1, 8, 512), axis=0)
        p = p[:, :128] + p[:, 128:256] + p[:, 256:384] + p[:, 384:]
        return jnp.sum(p, axis=0, keepdims=True)

    def inner(v):
        def step(i, carry):
            prod = v[y, zl, i].astype(F32) * acc[i]
            return carry + jnp.sum(prod.reshape(-1, 8, 512), axis=0)

        return row(lax.fori_loop(0, NZH, step, jnp.zeros((8, 512), F32)))

    def tile(parts):
        index = lax.broadcasted_iota(jnp.int32, (8, 128), 0)
        out = jnp.zeros((8, 128), F32)
        for i, p in enumerate(parts):
            out = jnp.where(index == i, jnp.broadcast_to(p, (8, 128)), out)
        return out

    def reduce_out(parts_of, left_to_wait):
        core = copy(acc.at[:, :, 1 - c], rs_core, RS_C, at(dc=1))
        core.start()
        sent = [core]
        ar1[z, c] = tile(parts_of())
        far = (4, 3, 5, 2, 6, 1, 7, 0)
        zc = [(dz, dc) for dz in far for dc in (0, 1) if dz or dc]
        xy = [(dx, dy) for dx in (2, 1, 3, 0) for dy in (2, 1, 3, 0) if dx or dy]
        for dz, dc in zc:
            cp = copy(ar1.at[z, c], ar1.at[z, c], AR1 + dz * NC + dc, at(dz=dz, dc=dc))
            cp.start()
            sent.append(cp)
        core.wait_recv()
        rs_core[...] = acc[:, :, c] + rs_core[...]
        rs_send[...] = rs_core[...].astype(BF16)
        zx = [(dzh, dx) for dzh in (2, 1, 3, 0) for dx in (2, 1, 3, 0) if dzh or dx]
        for dzh, dx in zx:
            slot = dzh * NX + dx
            cp = copy(
                rs_send.at[zhs[dzh * NZL], xs[dx]],
                rs_recv.at[slot],
                RS + slot,
                at(dx=dx, dz=dzh * NZL),
            )
            cp.start()
            sent.append(cp)
        for dz, dc in reversed(zc):
            other = ar1.at[zs[-dz % NZ], cs_[dc]]
            copy(other, other, AR1 + dz * NC + dc, at(dc=1)).wait_recv()
        ar2[x, y] = jnp.sum(ar1[...].reshape(NZ * NC, 8, 128), axis=0)
        for dx, dy in xy:
            cp = copy(ar2.at[x, y], ar2.at[x, y], AR2 + dx * NY + dy, at(dx=dx, dy=dy))
            cp.start()
            sent.append(cp)
        left_to_wait()
        result = rs_core[zh, x]
        for dzh, dx in reversed(zx):
            slot = dzh * NX + dx
            copy(rs_recv.at[slot], rs_recv.at[slot], RS + slot, at(dc=1)).wait_recv()
            result = result + rs_recv[slot].astype(F32)
        for dx, dy in reversed(xy):
            other = ar2.at[xs[-dx % NX], ys[-dy % NY]]
            copy(other, other, AR2 + dx * NY + dy, at(dc=1)).wait_recv()
        sums = jnp.sum(ar2[...].reshape(NX * NY, 8, 128), axis=0)

        def finish():
            for cp in sent:
                cp.wait_send()

        return result * valid, sums, finish

    def scalar(sums, i):
        return jnp.sum(sums[i : i + 1, :], axis=1, keepdims=True)

    left_to_wait = all_gather(v1)
    load_source.wait()
    load_left.wait()
    load_right.wait()
    apply_ops(v1)
    raw, sums, finish = reduce_out(
        lambda: [row(keep[0] * keep[0]), inner(v1)], left_to_wait
    )
    load_diag.wait()
    squares = scalar(sums, 0) / total
    scale = 1.0 / jnp.sqrt(squares + 1e-06)
    theta = scale * scale * scalar(sums, 1) / total
    first_vec = keep[0] * scale
    first_sigma = raw * scale
    correction = (first_sigma - theta * first_vec) / jnp.maximum(
        jnp.abs(diag_ref[0] - theta), 1.0
    )
    keep[1] = correction
    keep[2] = first_sigma
    keep[0] = first_vec
    v2[y, zl, zh, x, c] = correction.astype(BF16)

    left_to_wait = all_gather(v2)
    finish()
    apply_ops(v2)
    raw2, sums, finish = reduce_out(
        lambda: [
            row(keep[0] * keep[1]),
            row(keep[1] * keep[1]),
            row(keep[1] * keep[2]),
            inner(v1) * scale,
            inner(v2),
        ],
        left_to_wait,
    )
    first_sq = scale * scale * squares
    corre = scalar(sums, 0) / total
    corr_sq = scalar(sums, 1) / total
    corr_sigma = scalar(sums, 2) / total
    first_raw = scalar(sums, 3) / total
    corr_raw = scalar(sums, 4) / total
    orth_sq = jnp.maximum(corr_sq - 2.0 * corre * corre + corre * corre * first_sq, 0.0)
    norm = 1.0 / jnp.sqrt(orth_sq + 1e-06)
    vec_ref[0] = (keep[1] - corre * keep[0]) * norm
    sig_ref[0] = (raw2 - corre * keep[2]) * norm
    upper = (first_raw - corre * theta) * norm
    lower = (corr_sigma - corre * theta) * norm
    corner = (
        (corr_raw - corre * corr_sigma - corre * first_raw + corre * corre * theta)
        * norm
        * norm
    )
    r = lax.broadcasted_iota(jnp.int32, (2, 2), 0)
    q = lax.broadcasted_iota(jnp.int32, (2, 2), 1)
    low = jnp.where(q == 0, lower, corner)
    high = jnp.where(q == 0, theta, upper)
    sub_ref[...] = jnp.where(r == 0, high, low)
    finish()


def local(wave, left_ops, right_ops, diagonal, block_size, source):
    terms, _, width, _ = left_ops.shape
    total = float(block_size.shape[0] * width * width)
    vmem = pl.BlockSpec(memory_space=pltpu.VMEM)
    hbm = pl.BlockSpec(memory_space=pltpu.HBM)
    slab = (16, width)

    def body(*refs):
        kernel(total, *refs)

    vec, sig, sub = pl.pallas_call(
        body,
        out_shape=(
            jax.ShapeDtypeStruct((1,) + slab, F32),
            jax.ShapeDtypeStruct((1,) + slab, F32),
            jax.ShapeDtypeStruct((2, 2), F32),
        ),
        in_specs=[hbm] * 6,
        out_specs=(vmem, vmem, vmem),
        scratch_shapes=[
            pltpu.SMEM(block_size.shape, jnp.int32),
            pltpu.SMEM(source.shape, jnp.int32),
            pltpu.VMEM((1,) + slab, F32),
            pltpu.VMEM((1,) + slab, F32),
            pltpu.VMEM((terms, width, width), BF16),
            pltpu.VMEM((terms, width, width), BF16),
            pltpu.VMEM((NY, NZL, NZH, NX, NC) + slab, BF16),
            pltpu.VMEM((NY, NZL, NZH, NX, NC) + slab, BF16),
            pltpu.VMEM((NZH, NX, NC) + slab, F32),
            pltpu.VMEM((NZH, NX) + slab, F32),
            pltpu.VMEM((NZH, NX) + slab, BF16),
            pltpu.VMEM((NZH * NX,) + slab, BF16),
            pltpu.VMEM((NZ, NC, 8, 128), F32),
            pltpu.VMEM((NX, NY, 8, 128), F32),
            pltpu.VMEM((3,) + slab, F32),
            pltpu.SemaphoreType.DMA((NSEM,)),
            pltpu.SemaphoreType.DMA((NSEM,)),
            pltpu.SemaphoreType.DMA((6,)),
        ],
        compiler_params=pltpu.CompilerParams(
            collective_id=0, has_side_effects=True, vmem_limit_bytes=60 * 1024 * 1024
        ),
    )(block_size, source, wave, diagonal, left_ops, right_ops)

    def hand_out(vec_in, sig_in, sub_in, vec_out, sig_out, sub_out):
        vec_out[...] = vec_in[...]
        sig_out[...] = sig_in[...]
        sub_out[...] = sub_in[...]

    return pl.pallas_call(
        hand_out,
        out_shape=(
            jax.ShapeDtypeStruct(vec.shape, F32),
            jax.ShapeDtypeStruct(sig.shape, F32),
            jax.ShapeDtypeStruct(sub.shape, F32),
        ),
        in_specs=[vmem] * 3,
        out_specs=(vmem,) * 3,
    )(vec, sig, sub)


def solution(mesh):
    return jax.shard_map(
        local,
        mesh=mesh,
        in_specs=(
            P("sector", "term", None),
            P("term", "sector", None, None),
            P("term", "sector", None, None),
            P("sector", "term", None),
            P(),
            P("term", None),
        ),
        out_specs=(P("sector", "term", None), P("sector", "term", None), P()),
        check_vma=False,
    )
```

```python
import jax
import jax.numpy as jnp
from jax import lax
from jax.experimental import pallas as pl
from jax.experimental.pallas import tpu as pltpu
from jax.sharding import PartitionSpec as P

MESH = pl.DeviceIdType.MESH
F32 = jnp.float32
BF16 = jnp.bfloat16

NX, NY, NZH, NZL, NC = 4, 4, 4, 2, 2
NZ = NZH * NZL

TERMS_AT_ONCE = 8

AG_F2 = 0
AG_Z = 1
AG_Z2 = 8
AG_F = 15
AG_GR = 17
AG_GL = 21
AG_HR = 25
AG_HL = 29
AG_M = 33
RS_C = 49
RS = 50
AR1 = 66
AR2 = 82
NSEM = 98


def kernel(
    total,
    bs_hbm,
    source_hbm,
    wave_hbm,
    diag_hbm,
    left_hbm,
    right_hbm,
    vec_ref,
    sig_ref,
    sub_ref,
    bs_ref,
    source_ref,
    wave_ref,
    diag_ref,
    left,
    right,
    v1,
    v2,
    acc,
    rs_core,
    rs_send,
    rs_recv,
    ar1,
    ar2,
    keep,
    send,
    recv,
    local_sem,
):
    term = lax.axis_index("term")
    sector = lax.axis_index("sector")
    c = term % NC
    x = (term // NC) % NX
    zh = term // (NX * NC)
    y = sector // NZL
    zl = sector % NZL
    z = zh * NZL + zl
    terms = left.shape[0]

    xs = [x] + [(x + d) % NX for d in range(1, NX)]
    ys = [y] + [(y + d) % NY for d in range(1, NY)]
    zs = [z] + [(z + d) % NZ for d in range(1, NZ)]
    zhs = [zh] + [zz // NZL for zz in zs[1:]]
    zls = [zl, 1 - zl] * NZH
    cs_ = [c, 1 - c]

    def at(dx=0, dy=0, dz=0, dc=0):
        dx, dy, dz = dx % NX, dy % NY, dz % NZ
        return {
            "term": zhs[dz] * (NX * NC) + xs[dx] * NC + cs_[dc],
            "sector": ys[dy] * NZL + zls[dz],
        }

    def copy(src, dst, slot, dev):
        return pltpu.make_async_remote_copy(
            src_ref=src,
            dst_ref=dst,
            send_sem=send.at[slot],
            recv_sem=recv.at[slot],
            device_id=dev,
            device_id_type=MESH,
        )

    def load(src, dst, i):
        cp = pltpu.make_async_copy(src, dst, local_sem.at[i])
        cp.start()
        return cp

    barrier = pltpu.get_barrier_semaphore()
    peers = [at(dx=d) for d in (1, 2, 3)] + [at(dy=d) for d in (1, 2, 3)]
    peers += [at(dz=d) for d in range(1, NZ)] + [at(dc=1)]
    for dev in peers:
        pl.semaphore_signal(barrier, inc=1, device_id=dev, device_id_type=MESH)
    load_wave = load(wave_hbm, wave_ref, 0)
    load_bs = load(bs_hbm, bs_ref, 1)
    load_source = load(source_hbm, source_ref, 2)
    load_diag = load(diag_hbm, diag_ref, 3)
    load_left = load(left_hbm.at[:, 0], left, 4)
    load_right = load(right_hbm.at[:, 0], right, 5)

    load_bs.wait()
    load_wave.wait()
    rows = term * 16 + lax.broadcasted_iota(jnp.int32, (16, 512), 0)
    cols = lax.broadcasted_iota(jnp.int32, (16, 512), 1)
    size = bs_ref[sector]
    valid = ((rows < size) & (cols < size)).astype(F32)
    masked = wave_ref[0] * valid
    keep[0] = masked
    v1[y, zl, zh, x, c] = masked.astype(BF16)
    pl.semaphore_wait(barrier, len(peers))

    def gather(v, cs):
        fs, gs = (xs, ys) if cs == 0 else (ys, xs)
        every = slice(None)
        sent = []

        def piece(df, dz):
            i, j = (gs[0], fs[df % 4]) if cs == 0 else (fs[df % 4], gs[0])
            return v.at[i, zls[dz % NZ], zhs[dz % NZ], j, cs]

        def block(df, dg, part=every):
            i, j = (gs[dg % 4], fs[df % 4]) if cs == 0 else (fs[df % 4], gs[dg % 4])
            return v.at[i, :, part, j, cs]

        half_a, half_b = pl.ds(0, 2), pl.ds(2, 2)

        def dev_f(d):
            return at(dx=d) if cs == 0 else at(dy=d)

        def dev_g(d):
            return at(dy=d) if cs == 0 else at(dx=d)

        def go(slot, of, dev):
            copy(of(), of(), slot, dev).start()
            sent.append((slot, of))

        def got(slot, of):
            copy(of(), of(), slot, at(dc=1)).wait_recv()

        def mirror(df, dg):
            of = lambda: block(df, dg)
            go(AG_M + (df % 4) * 4 + dg % 4, of, at(dc=1))

        def g_send(df):
            go(AG_GR + df % 4, lambda: block(df, 0), dev_g(1))
            go(AG_GL + df % 4, lambda: block(df, 0), dev_g(-1))
            mirror(df, 0)

        def g_pass(df):
            got(AG_GR + df % 4, lambda: block(df, -1))
            go(AG_HR + df % 4, lambda: block(df, -1, half_a), dev_g(1))
            mirror(df, -1)
            got(AG_GL + df % 4, lambda: block(df, 1))
            go(AG_HL + df % 4, lambda: block(df, 1, half_b), dev_g(-1))
            mirror(df, 1)

        def g_end(df):
            got(AG_HR + df % 4, lambda: block(df, 2, half_a))
            got(AG_HL + df % 4, lambda: block(df, 2, half_b))
            mirror(df, 2)

        def z_send(df, slot):
            for d in (4, 3, 5, 2, 6, 1, 7):
                go(slot + d - 1, lambda: piece(df, 0), at(dz=d))

        def z_got(df, slot):
            for d in (1, 7, 2, 6, 3, 5, 4):
                got(slot + d - 1, lambda: piece(df, -d))

        def first():
            go(AG_F2, lambda: piece(0, 0), dev_f(2))
            z_send(0, AG_Z)

        def second():
            got(AG_F2, lambda: piece(2, 0))
            z_send(2, AG_Z2)

        def third():
            z_got(0, AG_Z)
            go(AG_F, lambda: block(0, 0), dev_f(1))
            go(AG_F + 1, lambda: block(0, 0), dev_f(-1))
            g_send(0)

        def fourth():
            z_got(2, AG_Z2)
            g_send(2)

        def fifth():
            got(AG_F, lambda: block(-1, 0))
            g_send(-1)
            got(AG_F + 1, lambda: block(1, 0))
            g_send(1)

        def pass_0():
            g_pass(0)

        def pass_2():
            g_pass(2)

        def pass_1():
            g_pass(-1)
            g_pass(1)

        def end_0():
            g_end(0)

        def end_2():
            g_end(2)

        def end_1():
            g_end(-1)
            g_end(1)

        def last():
            for i in range(16):
                got(AG_M + i, lambda: block(0, 0))

        def sent_all():
            for slot, of in sent:
                copy(of(), of(), slot, at(dc=1)).wait_send()

        arrive = [first, third, second, pass_0, fifth, fourth]
        arrive += [end_0, pass_1, pass_2, end_1, end_2, last]
        return arrive, sent_all

    def all_gather(v):
        steps = [gather(v, cs) for cs in range(NC)]

        def run(todo):
            for cs in range(NC):

                @pl.when(c == cs)
                def _(cs=cs):
                    for step in todo(*steps[cs]):
                        step()

        run(lambda arrive, sent_all: arrive)
        return lambda: run(lambda arrive, sent_all: [sent_all])

    def apply_ops(v):
        acc[...] = jnp.zeros_like(acc)

        def step(i, carry):
            halves, rights = [], []
            for k in range(TERMS_AT_ONCE):
                t = i * TERMS_AT_ONCE + k
                src = source_ref[t, sector]
                block = v[src >> 1, src & 1].reshape(512, 512)
                half = jnp.dot(left[t], block, preferred_element_type=F32)
                halves.append(half.astype(BF16))
                rights.append(right[t])
            part = lax.dot_general(
                jnp.concatenate(halves, axis=1),
                jnp.concatenate(rights, axis=1),
                (((1,), (1,)), ((), ())),
                preferred_element_type=F32,
            )
            acc[...] += part.reshape(acc.shape)
            return carry

        lax.fori_loop(0, terms // TERMS_AT_ONCE, step, 0)

    def row(p):
        p = jnp.sum(p.reshape(-1, 8, 512), axis=0)
        p = p[:, :128] + p[:, 128:256] + p[:, 256:384] + p[:, 384:]
        return jnp.sum(p, axis=0, keepdims=True)

    def inner(v):
        def step(i, carry):
            prod = v[y, zl, i].astype(F32) * acc[i]
            return carry + jnp.sum(prod.reshape(-1, 8, 512), axis=0)

        return row(lax.fori_loop(0, NZH, step, jnp.zeros((8, 512), F32)))

    def tile(parts):
        index = lax.broadcasted_iota(jnp.int32, (8, 128), 0)
        out = jnp.zeros((8, 128), F32)
        for i, p in enumerate(parts):
            out = jnp.where(index == i, jnp.broadcast_to(p, (8, 128)), out)
        return out

    def reduce_out(parts_of, left_to_wait):
        core = copy(acc.at[:, :, 1 - c], rs_core, RS_C, at(dc=1))
        core.start()
        sent = [core]
        ar1[z, c] = tile(parts_of())
        far = (4, 3, 5, 2, 6, 1, 7, 0)
        zc = [(dz, dc) for dz in far for dc in (0, 1) if dz or dc]
        xy = [(dx, dy) for dx in (2, 1, 3, 0) for dy in (2, 1, 3, 0) if dx or dy]
        for dz, dc in zc:
            cp = copy(ar1.at[z, c], ar1.at[z, c], AR1 + dz * NC + dc, at(dz=dz, dc=dc))
            cp.start()
            sent.append(cp)
        core.wait_recv()
        rs_core[...] = acc[:, :, c] + rs_core[...]
        rs_send[...] = rs_core[...].astype(BF16)
        zx = [(dzh, dx) for dzh in (2, 1, 3, 0) for dx in (2, 1, 3, 0) if dzh or dx]
        for dzh, dx in zx:
            slot = dzh * NX + dx
            cp = copy(
                rs_send.at[zhs[dzh * NZL], xs[dx]],
                rs_recv.at[slot],
                RS + slot,
                at(dx=dx, dz=dzh * NZL),
            )
            cp.start()
            sent.append(cp)
        for dz, dc in reversed(zc):
            other = ar1.at[zs[-dz % NZ], cs_[dc]]
            copy(other, other, AR1 + dz * NC + dc, at(dc=1)).wait_recv()
        ar2[x, y] = jnp.sum(ar1[...].reshape(NZ * NC, 8, 128), axis=0)
        for dx, dy in xy:
            cp = copy(ar2.at[x, y], ar2.at[x, y], AR2 + dx * NY + dy, at(dx=dx, dy=dy))
            cp.start()
            sent.append(cp)
        left_to_wait()
        result = rs_core[zh, x]
        for dzh, dx in reversed(zx):
            slot = dzh * NX + dx
            copy(rs_recv.at[slot], rs_recv.at[slot], RS + slot, at(dc=1)).wait_recv()
            result = result + rs_recv[slot].astype(F32)
        for dx, dy in reversed(xy):
            other = ar2.at[xs[-dx % NX], ys[-dy % NY]]
            copy(other, other, AR2 + dx * NY + dy, at(dc=1)).wait_recv()
        sums = jnp.sum(ar2[...].reshape(NX * NY, 8, 128), axis=0)

        def finish():
            for cp in sent:
                cp.wait_send()

        return result * valid, sums, finish

    def scalar(sums, i):
        return jnp.sum(sums[i : i + 1, :], axis=1, keepdims=True)

    left_to_wait = all_gather(v1)
    load_source.wait()
    load_left.wait()
    load_right.wait()
    apply_ops(v1)
    raw, sums, finish = reduce_out(
        lambda: [row(keep[0] * keep[0]), inner(v1)], left_to_wait
    )
    load_diag.wait()
    squares = scalar(sums, 0) / total
    scale = 1.0 / jnp.sqrt(squares + 1e-06)
    theta = scale * scale * scalar(sums, 1) / total
    first_vec = keep[0] * scale
    first_sigma = raw * scale
    correction = (first_sigma - theta * first_vec) / jnp.maximum(
        jnp.abs(diag_ref[0] - theta), 1.0
    )
    keep[1] = correction
    keep[2] = first_sigma
    keep[0] = first_vec
    v2[y, zl, zh, x, c] = correction.astype(BF16)

    left_to_wait = all_gather(v2)
    finish()
    apply_ops(v2)
    raw2, sums, finish = reduce_out(
        lambda: [
            row(keep[0] * keep[1]),
            row(keep[1] * keep[1]),
            row(keep[1] * keep[2]),
            inner(v1) * scale,
            inner(v2),
        ],
        left_to_wait,
    )
    first_sq = scale * scale * squares
    corre = scalar(sums, 0) / total
    corr_sq = scalar(sums, 1) / total
    corr_sigma = scalar(sums, 2) / total
    first_raw = scalar(sums, 3) / total
    corr_raw = scalar(sums, 4) / total
    orth_sq = jnp.maximum(corr_sq - 2.0 * corre * corre + corre * corre * first_sq, 0.0)
    norm = 1.0 / jnp.sqrt(orth_sq + 1e-06)
    vec_ref[0] = (keep[1] - corre * keep[0]) * norm
    sig_ref[0] = (raw2 - corre * keep[2]) * norm
    upper = (first_raw - corre * theta) * norm
    lower = (corr_sigma - corre * theta) * norm
    corner = (
        (corr_raw - corre * corr_sigma - corre * first_raw + corre * corre * theta)
        * norm
        * norm
    )
    r = lax.broadcasted_iota(jnp.int32, (2, 2), 0)
    q = lax.broadcasted_iota(jnp.int32, (2, 2), 1)
    low = jnp.where(q == 0, lower, corner)
    high = jnp.where(q == 0, theta, upper)
    sub_ref[...] = jnp.where(r == 0, high, low)
    finish()


def local(wave, left_ops, right_ops, diagonal, block_size, source):
    terms, _, width, _ = left_ops.shape
    total = float(block_size.shape[0] * width * width)
    vmem = pl.BlockSpec(memory_space=pltpu.VMEM)
    hbm = pl.BlockSpec(memory_space=pltpu.HBM)
    slab = (16, width)

    def body(*refs):
        kernel(total, *refs)

    vec, sig, sub = pl.pallas_call(
        body,
        out_shape=(
            jax.ShapeDtypeStruct((1,) + slab, F32),
            jax.ShapeDtypeStruct((1,) + slab, F32),
            jax.ShapeDtypeStruct((2, 2), F32),
        ),
        in_specs=[hbm] * 6,
        out_specs=(vmem, vmem, vmem),
        scratch_shapes=[
            pltpu.SMEM(block_size.shape, jnp.int32),
            pltpu.SMEM(source.shape, jnp.int32),
            pltpu.VMEM((1,) + slab, F32),
            pltpu.VMEM((1,) + slab, F32),
            pltpu.VMEM((terms, width, width), BF16),
            pltpu.VMEM((terms, width, width), BF16),
            pltpu.VMEM((NY, NZL, NZH, NX, NC) + slab, BF16),
            pltpu.VMEM((NY, NZL, NZH, NX, NC) + slab, BF16),
            pltpu.VMEM((NZH, NX, NC) + slab, F32),
            pltpu.VMEM((NZH, NX) + slab, F32),
            pltpu.VMEM((NZH, NX) + slab, BF16),
            pltpu.VMEM((NZH * NX,) + slab, BF16),
            pltpu.VMEM((NZ, NC, 8, 128), F32),
            pltpu.VMEM((NX, NY, 8, 128), F32),
            pltpu.VMEM((3,) + slab, F32),
            pltpu.SemaphoreType.DMA((NSEM,)),
            pltpu.SemaphoreType.DMA((NSEM,)),
            pltpu.SemaphoreType.DMA((6,)),
        ],
        compiler_params=pltpu.CompilerParams(
            collective_id=0, has_side_effects=True, vmem_limit_bytes=60 * 1024 * 1024
        ),
    )(block_size, source, wave, diagonal, left_ops, right_ops)

    def hand_out(vec_in, sig_in, sub_in, vec_out, sig_out, sub_out):
        vec_out[...] = vec_in[...]
        sig_out[...] = sig_in[...]
        sub_out[...] = sub_in[...]

    return pl.pallas_call(
        hand_out,
        out_shape=(
            jax.ShapeDtypeStruct(vec.shape, F32),
            jax.ShapeDtypeStruct(sig.shape, F32),
            jax.ShapeDtypeStruct(sub.shape, F32),
        ),
        in_specs=[vmem] * 3,
        out_specs=(vmem,) * 3,
    )(vec, sig, sub)


def solution(mesh):
    return jax.shard_map(
        local,
        mesh=mesh,
        in_specs=(
            P("sector", "term", None),
            P("term", "sector", None, None),
            P("term", "sector", None, None),
            P("sector", "term", None),
            P(),
            P("term", None),
        ),
        out_specs=(P("sector", "term", None), P("sector", "term", None), P()),
        check_vma=False,
    )
```
